512 devices in a mesh: pts: 64 (over x, z), cand: 8 (over y, core).
Axes of the slice: x: 4, y: 4, z: 16, core: 2. Of those that a mesh axis runs over, the one named last changes fastest.
Arguments:
- points: bfloat16 [32768, 4096], P('pts'), may hold values from -6 to 6
- weights: float32 [32768], P('pts'), may hold values from 0.25 to 4
- coverage: float32 [32768], P('pts'), may hold values from 0 to 1.5
- cand_index: int32 [2, 4096], P(None, 'pts'), may hold values from 0 to 511
- winners: int32 [2], replicated, may hold values from 0 to 4095
Outputs:
- gains: float32 [2, 4096], P(None, ('pts', 'cand'))
- final_cover: float32 [32768], P('pts')
The draws below stay inside these ranges and needn't reach their ends.
All inputs are finite; a program needn't handle non-finite values.
Results may differ from the reference program's by a relative error of at most 0.0003.
Values may be sent and summed in bfloat16 or wider, within the bound.
No kernel may reach another device: no remote copies, remote signals or barrier semaphores. Data moves between devices by JAX's collectives and lax.ppermute only.
A program may use at most 64 MiB of HBM per device.

```python
import math
import jax
import jax.numpy as jnp
from jax import lax

D = 4096
PTS_DEV = 512
CAND_DEV = 8
ITERS = 2
NPTS = 32768
CANDS = 4096
N_PTS = 64
N_CAND = 8


def touch_ends(entries, rng, low, largest):
    longest = entries.shape.index(max(entries.shape))
    spots = []
    for shift in (0, 1):
        where = [jax.random.randint(jax.random.fold_in(rng, axis), (), 0, length) for axis, length in enumerate(entries.shape)]
        where[longest] = (where[longest] + shift) % entries.shape[longest]
        spots.append(tuple(where))
    return entries.at[spots[0]].set(low).at[spots[1]].set(largest)


def shard_levels(rng, extent, cuts, low, largest):
    factor_of = 1.0
    for position, parts in cuts:
        draws = jax.random.uniform(jax.random.fold_in(jax.random.fold_in(rng, 6), position), (parts,), jnp.float32, low / len(cuts), largest / len(cuts))
        factor_of = factor_of * jnp.repeat(jnp.exp(draws), extent[position] // parts).reshape((-1,) + (1,) * (len(extent) - 1 - position))
    return factor_of


def scatter_about(stream_key, extent, width, reach, shards=(), kind=jnp.bfloat16):
    array = width * jax.random.normal(stream_key, extent, jnp.float32)
    if shards:
        array = array * shard_levels(stream_key, extent, shards, -0.22, 0.18)
    return jnp.clip(array, -reach, reach).astype(kind)


def setup_inputs(seed: int = 0) -> dict:
    arg_keys = jax.random.split(jax.random.key(seed), 6)
    return {
        "points": scatter_about(arg_keys[0], (NPTS, D), 1.0, 6.0, ((0, 64),)),
        "weights": jnp.clip(jnp.exp(math.log(4.0) - 2.7725887 * jax.random.uniform(arg_keys[1], (NPTS,), jnp.float32) ** shard_levels(arg_keys[1], (NPTS,), ((0, 64),), -0.2, 0.2)), 0.25, 4.0),
        "coverage": jnp.clip(1.5 * jax.random.uniform(arg_keys[2], (NPTS,), jnp.float32) ** shard_levels(arg_keys[2], (NPTS,), ((0, 64),), -0.2, 0.2), 0.0, 1.5),
        "cand_index": touch_ends(jax.random.randint(arg_keys[3], (ITERS, CANDS), 0, PTS_DEV), jax.random.fold_in(arg_keys[3], 1), 0, PTS_DEV - 1).astype(jnp.int32),
        "winners": jax.random.randint(arg_keys[4], (ITERS,), 0, CANDS).astype(jnp.int32),
    }


def shard_gain(total, block, cands, scale):
    rows_blk, weight_blk, cover_blk = block
    sim = lax.dot_general(rows_blk, cands, (((1,), (1,)), ((), ())), preferred_element_type=jnp.float32) * scale
    term = jnp.sum(weight_blk[:, None] * jnp.maximum(sim - cover_blk[:, None], jnp.float32(0.0)), axis=0)
    return total + term, None


def reference(points, weights, coverage, cand_index, winners):
    scale = jnp.float32(D ** -0.5)
    per_row = CAND_DEV * N_CAND
    column = jnp.arange(CANDS, dtype=jnp.int32)
    owner = (column // per_row).astype(jnp.int32)
    rows = (owner[None, :] * PTS_DEV + cand_index).astype(jnp.int32)
    cover = coverage
    blocked_points = points.reshape(N_PTS, PTS_DEV, D)
    blocked_weights = weights.reshape(N_PTS, PTS_DEV)
    results = []
    for step in range(ITERS):
        cands = jnp.take(points, rows[step], axis=0)
        blocked_cover = cover.reshape(N_PTS, PTS_DEV)
        total, _ = lax.scan(lambda c, b: shard_gain(c, b, cands, scale), jnp.zeros((CANDS,), jnp.float32), (blocked_points, blocked_weights, blocked_cover))
        results.append(total / NPTS)
        chosen = jnp.take(points, rows[step][winners[step]][None], axis=0)
        sim = lax.dot_general(points, chosen, (((1,), (1,)), ((), ())), preferred_element_type=jnp.float32)[:, 0] * scale
        cover = jnp.maximum(cover, sim)
    return jnp.stack(results), cover
```

```python
import jax
import jax.numpy as jnp
from jax import lax
from jax.sharding import Mesh
from jax.sharding import PartitionSpec as P

PTS = ("pts_0", "pts_1")
PTS_CAND = ("pts_0", "pts_1", "cand")
LIFT = 2.0**13


def body(points, weights, coverage, cand_index, winners):
    rows_dev, width = points.shape
    steps, per_row = cand_index.shape
    n_x, n_z = (lax.axis_size(axis) for axis in PTS)
    n_cand = lax.axis_size("cand")
    per_dev = per_row // n_cand
    held = steps * per_dev
    total = float(rows_dev * n_x * n_z)
    scale = width ** (-0.5) / LIFT
    my_cand = lax.axis_index("cand")
    my_pts = lax.axis_index(PTS)

    mine = lax.dynamic_slice_in_dim(cand_index, my_cand * per_dev, per_dev, 1).reshape(-1)
    owner = winners // per_row
    won = jnp.take_along_axis(cand_index, (winners % per_row)[:, None], axis=1)[:, 0]
    won = jnp.where(owner == my_pts, won, -1)
    wanted = jnp.concatenate([mine, won])
    pick = jnp.where(
        wanted[:, None] == lax.broadcasted_iota(jnp.int32, (held + steps, rows_dev), 1), LIFT, 0.0
    ).astype(points.dtype)
    picked = lax.dot_general(
        pick, points, (((1,), (0,)), ((), ())), preferred_element_type=jnp.float32
    ).astype(jnp.float16)
    piece = steps * width // held
    sent = jnp.concatenate([picked[:held], picked[held:].reshape(held, piece)], axis=1)

    along_z = lax.all_gather(sent, PTS[1], axis=0, tiled=True)
    owner_x, owner_z = owner // n_z, owner % n_z
    part = held // steps
    chosen = [
        lax.dynamic_slice(along_z, (owner_z[t] * held + t * part, width), (part, piece)).reshape(1, width)
        for t in range(steps)
    ]
    pad = jnp.zeros((8 - steps, width), jnp.float16)
    column = jnp.concatenate([along_z[:, :width], *chosen, pad], axis=0)
    column_rows = n_z * held + 8
    block = lax.all_gather(column, PTS[0], axis=0, tiled=True).astype(points.dtype)
    block = block.reshape(n_x, column_rows, width)
    chosen = jnp.concatenate(
        [
            lax.dynamic_slice(block, (owner_x[t], n_z * held + t, 0), (1, 1, width))[0]
            for t in range(steps)
        ]
    )

    near = (
        lax.dot_general(points, chosen, (((1,), (1,)), ((), ())), preferred_element_type=jnp.float32)
        * scale
    )
    covers = [coverage]
    for t in range(steps):
        covers.append(jnp.maximum(covers[-1], near[:, t]))
    step_of = lax.broadcasted_iota(jnp.int32, (1, 1, n_z * held), 2) % held // per_dev
    cover = covers[0][:, None, None]
    for t in range(1, steps):
        cover = jnp.where(step_of >= t, covers[t][:, None, None], cover)
    sim = (
        lax.dot_general(
            points,
            block[:, : n_z * held],
            (((1,), (2,)), ((), ())),
            preferred_element_type=jnp.float32,
        )
        * scale
    )
    part = jnp.sum(weights[:, None, None] * jnp.maximum(sim - cover, 0.0), axis=0)
    part = lax.all_to_all(part.reshape(n_x * n_z, held), PTS, 0, 0, tiled=True)
    gains = jnp.sum(part, axis=0) / total
    return gains.reshape(steps, per_dev), covers[-1]


def solution(mesh):
    torus = Mesh(mesh.devices.reshape(4, 16, mesh.shape["cand"]), ("pts_0", "pts_1", "cand"))
    in_specs = (P(PTS, None), P(PTS), P(PTS), P(None, PTS), P())
    out_specs = (P(None, PTS_CAND), P(PTS))
    return jax.shard_map(body, mesh=torus, in_specs=in_specs, out_specs=out_specs, check_vma=False)
```

```python
import jax
import jax.numpy as jnp
from jax import lax
from jax.sharding import Mesh
from jax.sharding import PartitionSpec as P

PTS = ("pts_0", "pts_1")
PTS_CAND = ("pts_0", "pts_1", "cand")
WIRE = jnp.float16
LIFT = 2.0**13


def dot(a, b):
    return lax.dot_general(a, b, (((1,), (1,)), ((), ())), preferred_element_type=jnp.float32)


def body(points, weights, coverage, cand_index, winners):
    rows_dev, width = points.shape
    steps, per_row = cand_index.shape
    n_x, n_z = (lax.axis_size(axis) for axis in PTS)
    n_cand = lax.axis_size("cand")
    per_dev = per_row // n_cand
    total = float(rows_dev * n_x * n_z)
    scale = width ** (-0.5) / LIFT
    my_cand = lax.axis_index("cand")
    my_step = lax.axis_index(PTS[0]) % steps
    my_core = my_cand % 2
    half = rows_dev // 2

    beside = [(x, x ^ 1) for x in range(n_x)]
    twin = [(c, c ^ 1) for c in range(n_cand)]
    there = lax.ppermute(jnp.stack([weights, coverage]), PTS[0], beside)
    near_half = lax.ppermute(
        lax.dynamic_slice_in_dim(points, my_core * half, half, 0), PTS[0], beside
    )
    far_half = lax.ppermute(near_half, "cand", twin)

    mine = lax.dynamic_slice_in_dim(cand_index, my_cand * per_dev, per_dev, 1).reshape(-1)
    owner = winners // per_row
    won = jnp.take_along_axis(cand_index, (winners % per_row)[:, None], axis=1)[:, 0]
    won = jnp.where(owner == lax.axis_index(PTS), won, -1)
    wanted = jnp.concatenate([mine, won])
    held = steps * per_dev
    pick = jnp.where(
        wanted[:, None] == lax.broadcasted_iota(jnp.int32, (held + steps, rows_dev), 1), LIFT, 0.0
    ).astype(points.dtype)
    picked = lax.dot_general(
        pick, points, (((1,), (0,)), ((), ())), preferred_element_type=jnp.float32
    ).astype(WIRE)
    owner_x, owner_z = owner // n_z, owner % n_z

    piece = steps * width // per_dev
    wins = picked[held:].reshape(per_dev, piece)
    sent = [
        jnp.concatenate([picked[t * per_dev : (t + 1) * per_dev], wins], axis=1)
        for t in range(steps)
    ]
    sent = jnp.stack([sent[x % steps] for x in range(n_x)])
    along_x = lax.all_to_all(sent, PTS[0], 0, 0, tiled=True)
    part = per_dev // steps
    slots = n_x * per_dev
    wins = jnp.concatenate(
        [
            lax.dynamic_slice(along_x, (owner_x[t], t * part, width), (1, part, piece)).reshape(
                slots // steps, steps * width // slots
            )
            for t in range(steps)
        ]
    )
    column = jnp.concatenate([along_x[:, :, :width].reshape(slots, width), wins], axis=1)
    along_z = lax.all_gather(column, PTS[1], axis=0, tiled=True)
    along_z, there = lax.optimization_barrier((along_z, there))
    piece = steps * width // slots
    part = slots // steps
    chosen = jnp.concatenate(
        [
            lax.dynamic_slice(
                along_z, (owner_z[t] * slots + t * part, width), (part, piece)
            ).reshape(1, width)
            for t in range(steps)
        ]
    ).astype(points.dtype)
    block = along_z[:, :width].astype(points.dtype)

    covers = [coverage]
    near = dot(points, chosen) * scale
    for t in range(steps):
        covers.append(jnp.maximum(covers[-1], near[:, t]))

    def gain(rows, weight, cover):
        return jnp.sum(
            weight[:, None] * jnp.maximum(dot(rows, block) * scale - cover[:, None], 0.0), axis=0
        )

    def gain_there(rows, core):
        weight = lax.dynamic_slice_in_dim(there[0], core * half, half)
        cover = lax.dynamic_slice_in_dim(there[1], core * half, half)
        later = jnp.maximum(cover, dot(rows, chosen[:1])[:, 0] * scale)
        return gain(rows, weight, jnp.where(my_step == 0, cover, later))

    part = gain(points, weights, jnp.where(my_step == 0, covers[0], covers[1]))
    part = part + gain_there(near_half, my_core) + gain_there(far_half, 1 - my_core)
    part = part.reshape(n_z, n_x, per_dev).transpose(1, 0, 2).reshape(n_x * n_z, per_dev)
    part = lax.all_to_all(part, PTS, 0, 0, tiled=True)
    part = part.reshape(n_x // steps, steps, n_z, per_dev)
    return jnp.sum(part, axis=(0, 2)) / total, covers[-1]


def solution(mesh):
    torus = Mesh(mesh.devices.reshape(4, 16, mesh.shape["cand"]), ("pts_0", "pts_1", "cand"))
    in_specs = (P(PTS, None), P(PTS), P(PTS), P(None, PTS), P())
    out_specs = (P(None, PTS_CAND), P(PTS))
    return jax.shard_map(body, mesh=torus, in_specs=in_specs, out_specs=out_specs, check_vma=False)
```

```python
import jax
import jax.numpy as jnp
from jax import lax
from jax.sharding import Mesh
from jax.sharding import PartitionSpec as P

PTS = ("pts_0", "pts_1")
PTS_CAND = ("pts_0", "pts_1", "cand")
WIRE = jnp.float16
LIFT = 2.0**13


def dot(a, b):
    return lax.dot_general(a, b, (((1,), (1,)), ((), ())), preferred_element_type=jnp.float32)


def body(points, weights, coverage, cand_index, winners):
    rows_dev, width = points.shape
    steps, per_row = cand_index.shape
    n_x, n_z = (lax.axis_size(axis) for axis in PTS)
    n_cand = lax.axis_size("cand")
    per_dev = per_row // n_cand
    total = float(rows_dev * n_x * n_z)
    scale = width ** (-0.5) / LIFT
    my_cand = lax.axis_index("cand")
    my_step = lax.axis_index(PTS[0]) % steps
    my_core = my_cand % 2
    half = rows_dev // 2

    beside = [(x, x ^ 1) for x in range(n_x)]
    twin = [(c, c ^ 1) for c in range(n_cand)]
    there = lax.ppermute(jnp.stack([weights, coverage]), PTS[0], beside)
    near_half = lax.ppermute(
        lax.dynamic_slice_in_dim(points, my_core * half, half, 0), PTS[0], beside
    )
    far_half = lax.ppermute(near_half, "cand", twin)

    mine = lax.dynamic_slice_in_dim(cand_index, my_cand * per_dev, per_dev, 1).reshape(-1)
    slot = lax.broadcasted_iota(jnp.int32, cand_index.shape, 1)
    column_of = slot + lax.axis_index(PTS) * per_row
    won = jnp.sum(jnp.where(column_of == winners[:, None], cand_index + 1, 0), axis=1) - 1
    wanted = jnp.concatenate([mine, won])
    held = steps * per_dev
    pick = jnp.where(
        wanted[:, None] == lax.broadcasted_iota(jnp.int32, (held + steps, rows_dev), 1), LIFT, 0.0
    ).astype(points.dtype)
    picked = lax.dot_general(
        pick, points, (((1,), (0,)), ((), ())), preferred_element_type=jnp.float32
    ).astype(WIRE)

    piece = steps * width // per_dev
    wins = picked[held:].reshape(per_dev, piece)
    sent = [
        jnp.concatenate([picked[t * per_dev : (t + 1) * per_dev], wins], axis=1)
        for t in range(steps)
    ]
    sent = jnp.stack([sent[x % steps] for x in range(n_x)])
    along_x = lax.all_to_all(sent, PTS[0], 0, 0, tiled=True)
    slots = n_x * per_dev
    wins = jnp.sum(along_x[:, :, width:].astype(jnp.float32), axis=0).astype(WIRE)
    wins = jnp.concatenate(
        [
            wins[t * (per_dev // steps) : (t + 1) * (per_dev // steps)].reshape(
                slots // steps, steps * width // slots
            )
            for t in range(steps)
        ]
    )
    column = jnp.concatenate([along_x[:, :, :width].reshape(slots, width), wins], axis=1)
    along_z = lax.all_gather(column, PTS[1], axis=0, tiled=True)
    along_z, there = lax.optimization_barrier((along_z, there))
    piece = steps * width // slots
    part = slots // steps
    chosen = jnp.concatenate(
        [
            sum(
                along_z[z * slots + t * part : z * slots + (t + 1) * part, width:].astype(jnp.float32)
                for z in range(n_z)
            ).reshape(1, width)
            for t in range(steps)
        ]
    ).astype(points.dtype)
    block = along_z[:, :width].astype(points.dtype)

    covers = [coverage]
    near = dot(points, chosen) * scale
    for t in range(steps):
        covers.append(jnp.maximum(covers[-1], near[:, t]))

    def gain(rows, weight, cover):
        return jnp.sum(
            weight[:, None] * jnp.maximum(dot(rows, block) * scale - cover[:, None], 0.0), axis=0
        )

    def gain_there(rows, core):
        weight = lax.dynamic_slice_in_dim(there[0], core * half, half)
        cover = lax.dynamic_slice_in_dim(there[1], core * half, half)
        later = jnp.maximum(cover, dot(rows, chosen[:1])[:, 0] * scale)
        return gain(rows, weight, jnp.where(my_step == 0, cover, later))

    part = gain(points, weights, jnp.where(my_step == 0, covers[0], covers[1]))
    part = part + gain_there(near_half, my_core) + gain_there(far_half, 1 - my_core)
    part = part.reshape(n_z, n_x, per_dev).transpose(1, 0, 2).reshape(n_x * n_z, per_dev)
    part = lax.all_to_all(part, PTS, 0, 0, tiled=True)
    part = part.reshape(n_x // steps, steps, n_z, per_dev)
    return jnp.sum(part, axis=(0, 2)) / total, covers[-1]


def solution(mesh):
    torus = Mesh(mesh.devices.reshape(4, 16, mesh.shape["cand"]), ("pts_0", "pts_1", "cand"))
    in_specs = (P(PTS, None), P(PTS), P(PTS), P(None, PTS), P())
    out_specs = (P(None, PTS_CAND), P(PTS))
    return jax.shard_map(body, mesh=torus, in_specs=in_specs, out_specs=out_specs, check_vma=False)
```

```python
import jax
import jax.numpy as jnp
from jax import lax
from jax.experimental import pallas as pl
from jax.experimental.pallas import tpu as pltpu
from jax.sharding import Mesh
from jax.sharding import PartitionSpec as P

PTS = ("pts_0", "pts_1")
PTS_CAND = ("pts_0", "pts_1", "cand")
WIRE = jnp.float16
LIFT = 2.0**13
SUBLANES = 8


def dot(a, b):
    return lax.dot_general(a, b, (((1,), (1,)), ((), ())), preferred_element_type=jnp.float32)


def fetch(points, cand_index, winners):
    rows_dev, width = points.shape
    half = rows_dev // 2
    steps, per_row = cand_index.shape
    n_x = lax.axis_size(PTS[0])
    per_dev = per_row // lax.axis_size("cand")
    held = steps * per_dev
    parts = per_dev // steps
    piece = width // parts

    def kernel(index_ref, winners_ref, points_ref, out_ref, half_ref, *scratch):
        tiles_ref, rows_ref, wins_ref, stage_ref, sems, half_sems = scratch
        at = pl.multiple_of(lax.axis_index("cand") % 2 * half, SUBLANES)
        half_in = pltpu.make_async_copy(
            points_ref.at[pl.ds(at, half)], stage_ref, half_sems.at[0]
        )
        half_out = pltpu.make_async_copy(stage_ref, half_ref, half_sems.at[1])
        first = lax.axis_index("cand") * per_dev
        here = lax.axis_index(PTS) * per_row
        within, copies = [], []
        for r in range(held + steps):
            if r < held:
                row = index_ref[r // per_dev, first + r % per_dev]
                within.append(row % SUBLANES)
            else:
                slot = winners_ref[r - held] - here
                owned = (slot >= 0) & (slot < per_row)
                row = index_ref[r - held, jnp.clip(slot, 0, per_row - 1)]
                within.append(jnp.where(owned, row % SUBLANES, -1))
            at = pl.multiple_of(row // SUBLANES * SUBLANES, SUBLANES)
            copies.append(
                pltpu.make_async_copy(
                    points_ref.at[pl.ds(at, SUBLANES)], tiles_ref.at[r], sems.at[r]
                )
            )
            copies[-1].start()
        half_in.start()
        sublane = lax.broadcasted_iota(jnp.int32, (SUBLANES, width), 0)
        for r in range(held + steps):
            if r == per_dev:
                half_in.wait()
                half_out.start()
            copies[r].wait()
            tile = tiles_ref[r].astype(jnp.float32)
            row = jnp.sum(jnp.where(sublane == within[r], tile, 0.0), axis=0, keepdims=True)
            if r < held:
                rows_ref[r : r + 1] = row
            else:
                for k in range(parts):
                    at = (r - held) * parts + k
                    wins_ref[at : at + 1] = row[:, k * piece : (k + 1) * piece]
        for x in range(n_x):
            rows = rows_ref[x % steps * per_dev : (x % steps + 1) * per_dev]
            out_ref[x, :, :width] = rows.astype(out_ref.dtype)
            out_ref[x, :, width:] = wins_ref[...].astype(out_ref.dtype)
        half_out.wait()

    smem, vmem, hbm = (
        pl.BlockSpec(memory_space=space) for space in (pltpu.SMEM, pltpu.VMEM, pl.ANY)
    )
    return pl.pallas_call(
        kernel,
        out_shape=[
            jax.ShapeDtypeStruct((n_x, per_dev, width + piece), points.dtype),
            jax.ShapeDtypeStruct((half, width), points.dtype),
        ],
        in_specs=[smem, smem, hbm],
        out_specs=[vmem, hbm],
        scratch_shapes=[
            pltpu.VMEM((held + steps, SUBLANES, width), points.dtype),
            pltpu.VMEM((held, width), jnp.float32),
            pltpu.VMEM((per_dev, piece), jnp.float32),
            pltpu.VMEM((half, width), points.dtype),
            pltpu.SemaphoreType.DMA((held + steps,)),
            pltpu.SemaphoreType.DMA((2,)),
        ],
    )(cand_index, winners, points)


def body(points, weights, coverage, cand_index, winners):
    rows_dev, width = points.shape
    steps, per_row = cand_index.shape
    n_x, n_z = (lax.axis_size(axis) for axis in PTS)
    n_cand = lax.axis_size("cand")
    per_dev = per_row // n_cand
    total = float(rows_dev * n_x * n_z)
    scale = width ** (-0.5) / LIFT
    my_cand = lax.axis_index("cand")
    my_step = lax.axis_index(PTS[0]) % steps
    my_core = my_cand % 2
    half = rows_dev // 2

    beside = [(x, x ^ 1) for x in range(n_x)]
    twin = [(c, c ^ 1) for c in range(n_cand)]
    there = lax.ppermute(jnp.stack([weights, coverage]), PTS[0], beside)
    rows, own_half = fetch(points, cand_index, winners)
    near_half = lax.ppermute(own_half, PTS[0], beside)
    far_half = lax.ppermute(near_half, "cand", twin)

    sent = (rows.astype(jnp.float32) * LIFT).astype(WIRE)
    along_x = lax.all_to_all(sent, PTS[0], 0, 0, tiled=True)
    slots = n_x * per_dev
    wins = jnp.sum(along_x[:, :, width:].astype(jnp.float32), axis=0).astype(WIRE)
    wins = jnp.concatenate(
        [
            wins[t * (per_dev // steps) : (t + 1) * (per_dev // steps)].reshape(
                slots // steps, steps * width // slots
            )
            for t in range(steps)
        ]
    )
    column = jnp.concatenate([along_x[:, :, :width].reshape(slots, width), wins], axis=1)
    along_z = lax.all_gather(column, PTS[1], axis=0, tiled=True)
    along_z, there = lax.optimization_barrier((along_z, there))
    piece = steps * width // slots
    part = slots // steps
    chosen = jnp.concatenate(
        [
            sum(
                along_z[z * slots + t * part : z * slots + (t + 1) * part, width:].astype(jnp.float32)
                for z in range(n_z)
            ).reshape(1, width)
            for t in range(steps)
        ]
    ).astype(points.dtype)
    block = along_z[:, :width].astype(points.dtype)

    covers = [coverage]
    near = dot(points, chosen) * scale
    for t in range(steps):
        covers.append(jnp.maximum(covers[-1], near[:, t]))

    def gain(rows, weight, cover):
        return jnp.sum(
            weight[:, None] * jnp.maximum(dot(rows, block) * scale - cover[:, None], 0.0), axis=0
        )

    def gain_there(rows, core):
        weight = lax.dynamic_slice_in_dim(there[0], core * half, half)
        cover = lax.dynamic_slice_in_dim(there[1], core * half, half)
        later = jnp.maximum(cover, dot(rows, chosen[:1])[:, 0] * scale)
        return gain(rows, weight, jnp.where(my_step == 0, cover, later))

    part = gain(points, weights, jnp.where(my_step == 0, covers[0], covers[1]))
    part = part + gain_there(near_half, my_core) + gain_there(far_half, 1 - my_core)
    part = part.reshape(n_z, n_x, per_dev).transpose(1, 0, 2).reshape(n_x * n_z, per_dev)
    part = lax.all_to_all(part, PTS, 0, 0, tiled=True)
    part = part.reshape(n_x // steps, steps, n_z, per_dev)
    return jnp.sum(part, axis=(0, 2)) / total, covers[-1]


def solution(mesh):
    torus = Mesh(mesh.devices.reshape(4, 16, mesh.shape["cand"]), ("pts_0", "pts_1", "cand"))
    in_specs = (P(PTS, None), P(PTS), P(PTS), P(None, PTS), P())
    out_specs = (P(None, PTS_CAND), P(PTS))
    return jax.shard_map(body, mesh=torus, in_specs=in_specs, out_specs=out_specs, check_vma=False)
```

```python
import jax
import jax.numpy as jnp
from jax import lax
from jax.experimental import pallas as pl
from jax.experimental.pallas import tpu as pltpu
from jax.sharding import Mesh
from jax.sharding import PartitionSpec as P

PTS = ("pts_0", "pts_1")
PTS_CAND = ("pts_0", "pts_1", "cand")
WIRE = jnp.float16
LIFT = 2.0**13
SUBLANES = 8


def dot(a, b):
    return lax.dot_general(a, b, (((1,), (1,)), ((), ())), preferred_element_type=jnp.float32)


def fetch(points, cand_index, winners):
    rows_dev, width = points.shape
    half = rows_dev // 2
    steps, per_row = cand_index.shape
    n_x = lax.axis_size(PTS[0])
    per_dev = per_row // lax.axis_size("cand")
    held = steps * per_dev
    parts = per_dev // steps
    piece = width // parts

    def kernel(index_ref, winners_ref, points_ref, out_ref, half_ref, *scratch):
        tiles_ref, rows_ref, wins_ref, stage_ref, sems, half_sems = scratch
        at = pl.multiple_of(lax.axis_index("cand") % 2 * half, SUBLANES)
        half_in = pltpu.make_async_copy(
            points_ref.at[pl.ds(at, half)], stage_ref, half_sems.at[0]
        )
        half_out = pltpu.make_async_copy(stage_ref, half_ref, half_sems.at[1])
        first = lax.axis_index("cand") * per_dev
        here = lax.axis_index(PTS) * per_row
        within, copies = [], []
        for r in range(held + steps):
            if r < held:
                row = index_ref[r // per_dev, first + r % per_dev]
                within.append(row % SUBLANES)
            else:
                slot = winners_ref[r - held] - here
                owned = (slot >= 0) & (slot < per_row)
                row = index_ref[r - held, jnp.clip(slot, 0, per_row - 1)]
                within.append(jnp.where(owned, row % SUBLANES, -1))
            at = pl.multiple_of(row // SUBLANES * SUBLANES, SUBLANES)
            copies.append(
                pltpu.make_async_copy(
                    points_ref.at[pl.ds(at, SUBLANES)], tiles_ref.at[r], sems.at[r]
                )
            )
            copies[-1].start()
        half_in.start()
        sublane = lax.broadcasted_iota(jnp.int32, (SUBLANES, width), 0)
        for r in range(held + steps):
            if r == per_dev:
                half_in.wait()
                half_out.start()
            copies[r].wait()
            tile = tiles_ref[r].astype(jnp.float32)
            row = jnp.sum(jnp.where(sublane == within[r], tile, 0.0), axis=0, keepdims=True)
            if r < held:
                rows_ref[r : r + 1] = row
            else:
                for k in range(parts):
                    at = (r - held) * parts + k
                    wins_ref[at : at + 1] = row[:, k * piece : (k + 1) * piece]
        for x in range(n_x):
            rows = rows_ref[x % steps * per_dev : (x % steps + 1) * per_dev]
            out_ref[x, :, :width] = rows.astype(out_ref.dtype)
            out_ref[x, :, width:] = wins_ref[...].astype(out_ref.dtype)
        half_out.wait()

    smem, vmem, hbm = (
        pl.BlockSpec(memory_space=space) for space in (pltpu.SMEM, pltpu.VMEM, pl.ANY)
    )
    return pl.pallas_call(
        kernel,
        out_shape=[
            jax.ShapeDtypeStruct((n_x, per_dev, width + piece), points.dtype),
            jax.ShapeDtypeStruct((half, width), points.dtype),
        ],
        in_specs=[smem, smem, hbm],
        out_specs=[vmem, hbm],
        scratch_shapes=[
            pltpu.VMEM((held + steps, SUBLANES, width), points.dtype),
            pltpu.VMEM((held, width), jnp.float32),
            pltpu.VMEM((per_dev, piece), jnp.float32),
            pltpu.VMEM((half, width), points.dtype),
            pltpu.SemaphoreType.DMA((held + steps,)),
            pltpu.SemaphoreType.DMA((2,)),
        ],
        compiler_params=pltpu.CompilerParams(vmem_limit_bytes=52 * 1024 * 1024),
    )(cand_index, winners, points)


def body(points, weights, coverage, cand_index, winners):
    rows_dev, width = points.shape
    steps, per_row = cand_index.shape
    n_x, n_z = (lax.axis_size(axis) for axis in PTS)
    n_cand = lax.axis_size("cand")
    per_dev = per_row // n_cand
    total = float(rows_dev * n_x * n_z)
    scale = width ** (-0.5) / LIFT
    my_cand = lax.axis_index("cand")
    my_step = lax.axis_index(PTS[0]) % steps
    my_core = my_cand % 2
    half = rows_dev // 2

    beside = [(x, x ^ 1) for x in range(n_x)]
    twin = [(c, c ^ 1) for c in range(n_cand)]
    there = lax.ppermute(jnp.stack([weights, coverage]), PTS[0], beside)
    rows, own_half = fetch(points, cand_index, winners)
    near_half = lax.ppermute(own_half, PTS[0], beside)
    far_half = lax.ppermute(near_half, "cand", twin)

    sent = (rows.astype(jnp.float32) * LIFT).astype(WIRE)
    along_x = lax.all_to_all(sent, PTS[0], 0, 0, tiled=True)
    slots = n_x * per_dev
    wins = jnp.sum(along_x[:, :, width:].astype(jnp.float32), axis=0).astype(WIRE)
    wins = jnp.concatenate(
        [
            wins[t * (per_dev // steps) : (t + 1) * (per_dev // steps)].reshape(
                slots // steps, steps * width // slots
            )
            for t in range(steps)
        ]
    )
    column = jnp.concatenate([along_x[:, :, :width].reshape(slots, width), wins], axis=1)
    along_z = lax.all_gather(column, PTS[1], axis=0, tiled=True)
    along_z, there = lax.optimization_barrier((along_z, there))
    piece = steps * width // slots
    part = slots // steps
    chosen = jnp.concatenate(
        [
            sum(
                along_z[z * slots + t * part : z * slots + (t + 1) * part, width:].astype(jnp.float32)
                for z in range(n_z)
            ).reshape(1, width)
            for t in range(steps)
        ]
    ).astype(points.dtype)
    block = along_z[:, :width].astype(points.dtype)

    covers = [coverage]
    near = dot(points, chosen) * scale
    for t in range(steps):
        covers.append(jnp.maximum(covers[-1], near[:, t]))

    def gain(rows, weight, cover):
        return jnp.sum(
            weight[:, None] * jnp.maximum(dot(rows, block) * scale - cover[:, None], 0.0), axis=0
        )

    def gain_there(rows, core):
        weight = lax.dynamic_slice_in_dim(there[0], core * half, half)
        cover = lax.dynamic_slice_in_dim(there[1], core * half, half)
        later = jnp.maximum(cover, dot(rows, chosen[:1])[:, 0] * scale)
        return gain(rows, weight, jnp.where(my_step == 0, cover, later))

    part = gain(points, weights, jnp.where(my_step == 0, covers[0], covers[1]))
    part = part + gain_there(near_half, my_core) + gain_there(far_half, 1 - my_core)
    part = part.reshape(n_z, n_x, per_dev).transpose(1, 0, 2).reshape(n_x * n_z, per_dev)
    part = lax.all_to_all(part, PTS, 0, 0, tiled=True)
    part = part.reshape(n_x // steps, steps, n_z, per_dev)
    return jnp.sum(part, axis=(0, 2)) / total, covers[-1]


def solution(mesh):
    torus = Mesh(mesh.devices.reshape(4, 16, mesh.shape["cand"]), ("pts_0", "pts_1", "cand"))
    in_specs = (P(PTS, None), P(PTS), P(PTS), P(None, PTS), P())
    out_specs = (P(None, PTS_CAND), P(PTS))
    return jax.shard_map(body, mesh=torus, in_specs=in_specs, out_specs=out_specs, check_vma=False)
```

```python
import jax
import jax.numpy as jnp
from jax import lax
from jax.experimental import pallas as pl
from jax.experimental.pallas import tpu as pltpu
from jax.sharding import Mesh
from jax.sharding import PartitionSpec as P

PTS = ("pts_0", "pts_1")
PTS_CAND = ("pts_0", "pts_1", "cand")
WIRE = jnp.float16
LIFT = 2.0**13
SUBLANES = 8


def dot(a, b):
    return lax.dot_general(a, b, (((1,), (1,)), ((), ())), preferred_element_type=jnp.float32)


def fetch(points, cand_index, winners):
    rows_dev, width = points.shape
    half = rows_dev // 2
    steps, per_row = cand_index.shape
    n_x = lax.axis_size(PTS[0])
    per_dev = per_row // lax.axis_size("cand")
    held = steps * per_dev
    parts = per_dev // steps
    piece = width // parts

    def kernel(index_ref, winners_ref, points_ref, out_ref, half_ref, *scratch):
        tiles_ref, rows_ref, wins_ref, stage_ref, sems, half_sems = scratch
        at = pl.multiple_of(lax.axis_index("cand") % 2 * half, SUBLANES)
        half_in = pltpu.make_async_copy(
            points_ref.at[pl.ds(at, half)], stage_ref, half_sems.at[0]
        )
        half_out = pltpu.make_async_copy(stage_ref, half_ref, half_sems.at[1])
        half_in.start()
        first = lax.axis_index("cand") * per_dev
        here = lax.axis_index(PTS) * per_row
        within, copies = [], []
        for r in range(held + steps):
            if r < held:
                row = index_ref[r // per_dev, first + r % per_dev]
                within.append(row % SUBLANES)
            else:
                slot = winners_ref[r - held] - here
                owned = (slot >= 0) & (slot < per_row)
                row = index_ref[r - held, jnp.clip(slot, 0, per_row - 1)]
                within.append(jnp.where(owned, row % SUBLANES, -1))
            at = pl.multiple_of(row // SUBLANES * SUBLANES, SUBLANES)
            copies.append(
                pltpu.make_async_copy(
                    points_ref.at[pl.ds(at, SUBLANES)], tiles_ref.at[r], sems.at[r]
                )
            )
            copies[-1].start()
        sublane = lax.broadcasted_iota(jnp.int32, (SUBLANES, width), 0)
        for r in range(held + steps):
            if r == per_dev:
                half_in.wait()
                half_out.start()
            copies[r].wait()
            tile = tiles_ref[r].astype(jnp.float32)
            row = jnp.sum(jnp.where(sublane == within[r], tile, 0.0), axis=0, keepdims=True)
            if r < held:
                rows_ref[r : r + 1] = row
            else:
                for k in range(parts):
                    at = (r - held) * parts + k
                    wins_ref[at : at + 1] = row[:, k * piece : (k + 1) * piece]
        for x in range(n_x):
            rows = rows_ref[x % steps * per_dev : (x % steps + 1) * per_dev]
            out_ref[x, :, :width] = rows.astype(out_ref.dtype)
            out_ref[x, :, width:] = wins_ref[...].astype(out_ref.dtype)
        half_out.wait()

    smem, vmem, hbm = (
        pl.BlockSpec(memory_space=space) for space in (pltpu.SMEM, pltpu.VMEM, pl.ANY)
    )
    return pl.pallas_call(
        kernel,
        out_shape=[
            jax.ShapeDtypeStruct((n_x, per_dev, width + piece), points.dtype),
            jax.ShapeDtypeStruct((half, width), points.dtype),
        ],
        in_specs=[smem, smem, hbm],
        out_specs=[vmem, hbm],
        scratch_shapes=[
            pltpu.VMEM((held + steps, SUBLANES, width), points.dtype),
            pltpu.VMEM((held, width), jnp.float32),
            pltpu.VMEM((per_dev, piece), jnp.float32),
            pltpu.VMEM((half, width), points.dtype),
            pltpu.SemaphoreType.DMA((held + steps,)),
            pltpu.SemaphoreType.DMA((2,)),
        ],
        compiler_params=pltpu.CompilerParams(vmem_limit_bytes=52 * 1024 * 1024),
    )(cand_index, winners, points)


def body(points, weights, coverage, cand_index, winners):
    rows_dev, width = points.shape
    steps, per_row = cand_index.shape
    n_x, n_z = (lax.axis_size(axis) for axis in PTS)
    n_cand = lax.axis_size("cand")
    per_dev = per_row // n_cand
    total = float(rows_dev * n_x * n_z)
    scale = width ** (-0.5) / LIFT
    my_cand = lax.axis_index("cand")
    my_step = lax.axis_index(PTS[0]) % steps
    my_core = my_cand % 2
    half = rows_dev // 2

    beside = [(x, x ^ 1) for x in range(n_x)]
    twin = [(c, c ^ 1) for c in range(n_cand)]
    there = lax.ppermute(jnp.stack([weights, coverage]), PTS[0], beside)
    rows, own_half = fetch(points, cand_index, winners)
    near_half = lax.ppermute(own_half, PTS[0], beside)
    far_half = lax.ppermute(near_half, "cand", twin)

    sent = (rows.astype(jnp.float32) * LIFT).astype(WIRE)
    along_x = lax.all_to_all(sent, PTS[0], 0, 0, tiled=True)
    slots = n_x * per_dev
    wins = jnp.sum(along_x[:, :, width:].astype(jnp.float32), axis=0).astype(WIRE)
    wins = jnp.concatenate(
        [
            wins[t * (per_dev // steps) : (t + 1) * (per_dev // steps)].reshape(
                slots // steps, steps * width // slots
            )
            for t in range(steps)
        ]
    )
    column = jnp.concatenate([along_x[:, :, :width].reshape(slots, width), wins], axis=1)
    along_z = lax.all_gather(column, PTS[1], axis=0, tiled=True)
    along_z, there = lax.optimization_barrier((along_z, there))
    piece = steps * width // slots
    part = slots // steps
    chosen = jnp.concatenate(
        [
            sum(
                along_z[z * slots + t * part : z * slots + (t + 1) * part, width:].astype(jnp.float32)
                for z in range(n_z)
            ).reshape(1, width)
            for t in range(steps)
        ]
    ).astype(points.dtype)
    block = along_z[:, :width].astype(points.dtype)

    covers = [coverage]
    near = dot(points, chosen) * scale
    for t in range(steps):
        covers.append(jnp.maximum(covers[-1], near[:, t]))

    def gain(rows, weight, cover):
        return jnp.sum(
            weight[:, None] * jnp.maximum(dot(rows, block) * scale - cover[:, None], 0.0), axis=0
        )

    def gain_there(rows, core):
        weight = lax.dynamic_slice_in_dim(there[0], core * half, half)
        cover = lax.dynamic_slice_in_dim(there[1], core * half, half)
        later = jnp.maximum(cover, dot(rows, chosen[:1])[:, 0] * scale)
        return gain(rows, weight, jnp.where(my_step == 0, cover, later))

    part = gain(points, weights, jnp.where(my_step == 0, covers[0], covers[1]))
    part = part + gain_there(near_half, my_core) + gain_there(far_half, 1 - my_core)
    part = part.reshape(n_z, n_x, per_dev).transpose(1, 0, 2).reshape(n_x * n_z, per_dev)
    part = lax.all_to_all(part, PTS, 0, 0, tiled=True)
    part = part.reshape(n_x // steps, steps, n_z, per_dev)
    return jnp.sum(part, axis=(0, 2)) / total, covers[-1]


def solution(mesh):
    torus = Mesh(mesh.devices.reshape(4, 16, mesh.shape["cand"]), ("pts_0", "pts_1", "cand"))
    in_specs = (P(PTS, None), P(PTS), P(PTS), P(None, PTS), P())
    out_specs = (P(None, PTS_CAND), P(PTS))
    return jax.shard_map(body, mesh=torus, in_specs=in_specs, out_specs=out_specs, check_vma=False)
```
